32 devices in a mesh: pack: 16 (over z, x, core), head: 2 (over y), rep: 1.
Axes of the slice: x: 2, y: 2, z: 4, core: 2. Of those that a mesh axis runs over, the one named last changes fastest.
Arguments:
- tokens: bfloat16 [49152, 1024], P(('rep', 'pack')), may hold values from -12 to 12
- ln_gain: float32 [1024], replicated, may hold values from 0.5 to 2
- attn_weight: bfloat16 [1024, 3, 1024], P(None, None, 'head'), may hold values from -6 to 6
- attn_proj: bfloat16 [1024, 1024], P('head'), may hold values from -0.1875 to 0.1875
- page_gain: float32 [1024], replicated, may hold values from 0.5 to 2
- page_weight: bfloat16 [1024, 3, 1024], P(None, None, 'head'), may hold values from -6 to 6
- page_proj: bfloat16 [1024, 1024], P('head'), may hold values from -0.1875 to 0.1875
- page_windows: int32 [48], P('rep'), may hold values from 1 to 12, 192 in all
- page_width: int32 [48], P('rep'), may hold values from 1 to 3
- doc_pages: int32 [12], P('rep'), may hold values from 1 to 8, 48 in all
Outputs:
- mixed: bfloat16 [49152, 1024], P(('rep', 'pack'), 'head')
- page_out: float32 [48, 1024], P('rep', 'head')
The draws below stay inside these ranges and needn't reach their ends.
Inputs may be any that keep to these rules, and one draw needn't show every extreme that they name: `page_windows`: the pages fill all 192 windows, and one page has exactly 12. `page_width`: A page's last row of windows may be short. `doc_pages`: the documents hold all 48 pages, and one has exactly 8.
All inputs are finite; a program needn't handle non-finite values.
Results may differ from the reference program's by a relative error of at most 0.03.
The reference program's roundings to bfloat16 on the way count: a program that leaves them out, or rounds other values in their place, can miss the bound.
Values may be sent and summed in bfloat16 or wider, within the bound.
A program may use at most 128 MiB of HBM per device.

```python
import math
import jax
import jax.numpy as jnp
import numpy as np
from jax import lax

D = 1024
HEADS = 32
WIN = 16
HALO = 4
PW_MAX = 3
PAGE_MOST = 12
WINDOWS = 192
TOKENS = 49152
PAGES = 48
DOCS = 12
DOC_MOST = 8


def draw_tokens(key, part):
    keys_all = jax.random.split(jax.random.fold_in(key, 11), 3)
    position = jnp.arange(TOKENS, dtype=jnp.float32)
    rising = 1.0 + 2.0 * position / TOKENS
    row_scale = jnp.exp(jax.random.uniform(keys_all[1], (TOKENS,), minval=math.log(0.1), maxval=0.0))
    col_scale = jnp.exp(jax.random.uniform(keys_all[2], (D,), minval=math.log(0.1), maxval=0.0))
    values_raw = jnp.clip(jax.random.normal(keys_all[0], (TOKENS, D)), -4.0, 4.0)
    return (values_raw * (rising * row_scale)[:, None] * col_scale[None, :]).astype(jnp.bfloat16)


def projection_draw(key, salt):
    keys_all = jax.random.split(jax.random.fold_in(key, salt), 1)
    entries = jnp.clip(jax.random.normal(keys_all[0], (D, 3, D)), -4.0, 4.0) / math.sqrt(D)
    return entries


def draw_attn_weight(key, part):
    return projection_draw(key, 21).astype(jnp.bfloat16)


def draw_page_weight(key, part):
    return projection_draw(key, 37).astype(jnp.bfloat16)


def place_ends(values, stream_key, least, high):
    spot = [jax.random.randint(jax.random.fold_in(stream_key, axis), (), 0, length) for axis, length in enumerate(values.shape)]
    longest = values.shape.index(max(values.shape))
    next_to = spot[:longest] + [(spot[longest] + 1) % values.shape[longest]] + spot[longest + 1:]
    return values.at[tuple(spot)].set(least).at[tuple(next_to)].set(high)


def block_scale(own_key, extent, cuts, least, largest):
    factor_of, own = 1.0, jax.random.fold_in(own_key, 6)
    for dim, blocks in cuts:
        draws = jnp.exp(jax.random.uniform(jax.random.fold_in(own, dim), (blocks,), jnp.float32, least / len(cuts), largest / len(cuts)))
        factor_of = factor_of * jnp.repeat(draws, extent[dim] // blocks).reshape([-1 if axis == dim else 1 for axis in range(len(extent))])
    return factor_of


def length_profile(number_of, total, most, lean):
    portions = [(1 << 20) // math.isqrt(rank ** lean) + 1 for rank in range(2, number_of + 1)]
    spare, holding = total - most - (number_of - 1), [1] * (number_of - 1)
    while spare > 0:
        movable = [i for i in range(number_of - 1) if holding[i] < most]
        whole, left = sum([portions[i] for i in movable]), spare
        for i in movable:
            extra = min(most - holding[i], max(1, left * portions[i] // whole), spare)
            holding[i] = holding[i] + extra
            spare = spare - extra
    return np.array([most] + holding)


def uneven(stream_key, count, total, reach, slope):
    if count == 2:
        one = jax.random.randint(stream_key, (), max(1, total - reach), min(reach, total - 1) + 1)
        return jnp.stack([one, total - one])
    tallies = jnp.asarray(length_profile(count, total, reach, slope), jnp.int32)
    couples = (count - 1) // 2
    giver, taker = tallies[1:1 + 2 * couples:2], tallies[2:2 + 2 * couples:2]
    margin = jnp.minimum(giver - 1, reach - taker)
    passed = jax.random.randint(jax.random.fold_in(stream_key, 1), (couples,), 0, 1 << 20) % (margin + 1)
    tallies = tallies.at[1:1 + 2 * couples:2].set(giver - passed).at[2:2 + 2 * couples:2].set(taker + passed)
    return tallies[jax.random.permutation(jax.random.fold_in(stream_key, 2), count)]


def gaussian(key, extent, deviation, bound, cuts=(), kind=jnp.bfloat16):
    loudness = block_scale(key, extent, cuts, -0.22, 0.18) if cuts else 1.0
    values = jax.random.normal(key, extent, jnp.float32) * deviation * loudness
    return jnp.minimum(jnp.maximum(values, -bound), bound).astype(kind)


def setup_inputs(seed: int = 0, part: int = 0) -> dict:
    splits = jax.random.split(jax.random.key(seed), 11)
    part_splits = jax.random.split(jax.random.fold_in(splits[10], part), 11)
    tokens = draw_tokens(jax.random.fold_in(jax.random.fold_in(splits[10], part), 71), part)
    ln_gain = jnp.clip(jnp.exp(jax.random.uniform(splits[1], (D,), jnp.float32, math.log(0.5), math.log(2.0))), 0.5, 2.0)
    attn_weight = draw_attn_weight(jax.random.fold_in(splits[10], 71), part)
    attn_proj = gaussian(splits[3], (D, D), D ** -0.5, 0.1875, ((0, 2),))
    page_gain = jnp.clip(jnp.exp(jax.random.uniform(splits[4], (D,), jnp.float32, math.log(0.5), math.log(2.0))), 0.5, 2.0)
    page_weight = draw_page_weight(jax.random.fold_in(splits[10], 71), part)
    page_proj = gaussian(splits[6], (D, D), D ** -0.5, 0.1875, ((0, 2),))
    page_windows = uneven(part_splits[7], PAGES, WINDOWS, PAGE_MOST, 2).astype(jnp.int32)
    page_width = place_ends(jax.random.randint(part_splits[8], (PAGES,), 1, PW_MAX + 1), jax.random.fold_in(part_splits[8], 1), 1, PW_MAX).astype(jnp.int32)
    doc_pages = uneven(part_splits[9], DOCS, PAGES, DOC_MOST, 1).astype(jnp.int32)
    return dict(tokens=tokens, ln_gain=ln_gain, attn_weight=attn_weight, attn_proj=attn_proj, page_gain=page_gain, page_weight=page_weight, page_proj=page_proj, page_windows=page_windows, page_width=page_width, doc_pages=doc_pages)


EPS = 1e-05
OFFSETS = ((-1, -1), (-1, 0), (-1, 1), (0, -1), (0, 0), (0, 1), (1, -1), (1, 0), (1, 1))

def layer_norm(values, gain):
    values = values.astype(jnp.float32)
    center = values - lax.optimization_barrier(jnp.mean(values, axis=-1, keepdims=True))
    spread = lax.optimization_barrier(jnp.mean(center * center, axis=-1, keepdims=True))
    return (center * lax.rsqrt(spread + EPS) * gain.astype(jnp.float32)).astype(jnp.bfloat16)

def page_member(window_ids, page_windows):
    page_ends = jnp.cumsum(page_windows).astype(jnp.int32)
    page_starts = (page_ends - page_windows).astype(jnp.int32)
    return (window_ids[:, None] >= page_starts[None, :]) & (window_ids[:, None] < page_ends[None, :])

def window_geometry(window_ids, page_windows, page_width):
    page_ends = jnp.cumsum(page_windows).astype(jnp.int32)
    page_starts = (page_ends - page_windows).astype(jnp.int32)
    member = page_member(window_ids, page_windows).astype(jnp.int32)
    begin = lax.optimization_barrier(jnp.sum(member * page_starts[None, :], axis=1)).astype(jnp.int32)
    across = lax.optimization_barrier(jnp.sum(member * page_width[None, :], axis=1)).astype(jnp.int32)
    total = lax.optimization_barrier(jnp.sum(member * page_windows[None, :], axis=1)).astype(jnp.int32)
    inside = window_ids - begin
    grid_row = inside // across
    grid_col = inside - grid_row * across
    rows_near = jnp.stack([grid_row + pair[0] for pair in OFFSETS], axis=1)
    cols_near = jnp.stack([grid_col + pair[1] for pair in OFFSETS], axis=1)
    place = rows_near * across[:, None] + cols_near
    valid = (cols_near >= 0) & (cols_near < across[:, None]) & (rows_near >= 0) & (place < total[:, None])
    return ((begin[:, None] + place).astype(jnp.int32), valid)

def gather_keys(extended, tile_index, valid):
    count = tile_index.shape[0]
    feats = extended.shape[-1]
    tiles = extended[tile_index]
    tiles = tiles.reshape(count, 3, 3, WIN, WIN, feats).transpose(0, 1, 3, 2, 4, 5).reshape(count, 3 * WIN, 3 * WIN, feats)
    lower_edge = WIN - HALO
    upper_edge = 2 * WIN + HALO
    region = tiles[:, lower_edge:upper_edge, lower_edge:upper_edge].reshape(count, -1, feats)
    grid_keep = jnp.broadcast_to(valid.reshape(count, 3, 1, 3, 1), (count, 3, WIN, 3, WIN)).reshape(count, 3 * WIN, 3 * WIN)
    keep = grid_keep[:, lower_edge:upper_edge, lower_edge:upper_edge].reshape(count, -1)
    return (region, keep)

def attention(query, keys, values, mask, heads):
    count, qlen, width = query.shape
    depth = width // heads
    q_heads = query.astype(jnp.float32).reshape(count, qlen, heads, depth)
    k_heads = keys.astype(jnp.float32).reshape(count, -1, heads, depth)
    v_heads = values.astype(jnp.float32).reshape(count, -1, heads, depth)
    scores = jnp.einsum('nqhd,nkhd->nhqk', q_heads, k_heads) / math.sqrt(depth)
    scores = jnp.where(mask[:, None], scores, -1e+30)
    top_score = lax.optimization_barrier(jnp.max(scores, axis=-1, keepdims=True))
    weights = jnp.exp(scores - top_score)
    probs = (weights / lax.optimization_barrier(jnp.sum(weights, axis=-1, keepdims=True))).astype(jnp.bfloat16)
    output = jnp.einsum('nhqk,nkhd->nqhd', probs.astype(jnp.float32), v_heads)
    return output.reshape(count, qlen, width).astype(jnp.bfloat16)

def reference(tokens, ln_gain, attn_weight, attn_proj, page_gain, page_weight, page_proj, page_windows, page_width, doc_pages):
    normed = layer_norm(tokens, ln_gain)
    qkv = jnp.dot(normed, attn_weight.reshape(D, 3 * D), preferred_element_type=jnp.float32).astype(jnp.bfloat16)
    queries = qkv[:, :D].reshape(WINDOWS, WIN * WIN, D)
    keyvals = qkv[:, D:].reshape(WINDOWS, WIN * WIN, 2 * D)
    window_ids = jnp.arange(WINDOWS, dtype=jnp.int32)
    neighbor, valid = window_geometry(window_ids, page_windows, page_width)
    tile_index = jnp.where(valid, neighbor, window_ids[:, None]).astype(jnp.int32)

    def attend(block):
        query_block, index_block, valid_block = block
        region, keep = gather_keys(keyvals, index_block, valid_block)
        return attention(query_block, region[..., :D], region[..., D:], keep[:, None, :], HEADS)
    mixed = lax.map(attend, (queries.reshape(WINDOWS, 1, WIN * WIN, D), tile_index.reshape(WINDOWS, 1, 9), valid.reshape(WINDOWS, 1, 9)))
    mixed = mixed.reshape(TOKENS, D)
    member = page_member(window_ids, page_windows).astype(jnp.float32)
    token_sums = lax.optimization_barrier(jnp.sum(tokens.reshape(WINDOWS, WIN * WIN, D), axis=1, dtype=jnp.float32))
    mixed_sums = lax.optimization_barrier(jnp.sum(mixed.reshape(WINDOWS, WIN * WIN, D), axis=1, dtype=jnp.float32))
    page_tokens = jnp.dot(member.T, token_sums, precision=lax.Precision.HIGHEST)
    page_mixed = jnp.dot(member.T, mixed_sums, precision=lax.Precision.HIGHEST)
    projected = jnp.dot(page_mixed, attn_proj.astype(jnp.float32), precision=lax.Precision.HIGHEST)
    counts = WIN * WIN * page_windows.astype(jnp.float32)
    pooled = (page_tokens + projected) / counts[:, None]
    page_normed = layer_norm(pooled, page_gain)
    page_qkv = jnp.dot(page_normed, page_weight.reshape(D, 3 * D), preferred_element_type=jnp.float32).astype(jnp.bfloat16)
    doc_ends = jnp.cumsum(doc_pages).astype(jnp.int32)
    page_ids = jnp.arange(PAGES, dtype=jnp.int32)
    doc_of = lax.optimization_barrier(jnp.sum((page_ids[:, None] >= doc_ends[None, :]).astype(jnp.int32), axis=1))
    same_doc = doc_of[:, None] == doc_of[None, :]
    context = attention(page_qkv[None, :, :D], page_qkv[None, :, D:2 * D], page_qkv[None, :, 2 * D:], same_doc[None], HEADS)[0]
    page_out = pooled + jnp.dot(context, page_proj, preferred_element_type=jnp.float32)
    return (mixed, page_out)
```

```python
import math

import jax
import jax.numpy as jnp
import numpy as np
from jax import lax
from jax.experimental import pallas as pl
from jax.experimental.pallas import tpu as pltpu
from jax.sharding import PartitionSpec as P

D = 1024
HDIM = 32
WIN = 16
HALO = 4
HALO_WIN = 4
TOK = WIN * WIN
STRIP = WIN * HALO
CORNER = HALO * HALO
SIDE_KEYS = 4 * STRIP + 4 * CORNER
KEYS = TOK + SIDE_KEYS
SIDE_LANES = 384
EPS = 1e-05
LOG2E = 1.4426950408889634
OFFSETS = ((-1, 0), (1, 0), (0, -1), (0, 1), (-1, -1), (-1, 1), (1, -1), (1, 1))


def near(offset_value):
    if offset_value < 0:
        return range(WIN - HALO, WIN)
    if offset_value > 0:
        return range(0, HALO)
    return range(0, WIN)


def strip_tokens():
    return [[r * WIN + c for r in near(a) for c in near(b)] for a, b in OFFSETS]


def one_hot(rows, width):
    table = np.zeros((SIDE_KEYS, width), np.float32)
    for i, j in enumerate(rows):
        if j >= 0:
            table[i, j] = 1.0
    padded = np.zeros((width, SIDE_LANES), np.float32)
    padded[:, :SIDE_KEYS] = table.T
    return jnp.asarray(table, jnp.bfloat16), jnp.asarray(padded, jnp.bfloat16)


def selections():
    strips = strip_tokens()
    flat = [t for s in strips for t in s]
    own = one_hot(flat, TOK)
    out = [own]
    for row_piece, col_piece in ((0, 2), (1, 3)):
        where = {t: i for i, t in enumerate(strips[row_piece])}
        cols = {t: STRIP + i for i, t in enumerate(strips[col_piece])}
        rows = []
        for number, strip in enumerate(strips):
            same = OFFSETS[number][0] == OFFSETS[row_piece][0]
            for t in strip:
                if same:
                    rows.append(where[t])
                elif number == col_piece:
                    rows.append(cols[t])
                else:
                    rows.append(-1)
        out.append(one_hot(rows, 2 * STRIP))
    return out


def nt_dot(a, b):
    return lax.dot_general(a, b, (((1,), (1,)), ((), ())), preferred_element_type=jnp.float32)


def nn_dot(a, b):
    return jnp.dot(a, b, preferred_element_type=jnp.float32)


def normalize(values, gain):
    center = values - jnp.mean(values, axis=-1, keepdims=True)
    spread = jnp.mean(center * center, axis=-1, keepdims=True)
    return (center * lax.rsqrt(spread + EPS) * gain).astype(jnp.bfloat16)


def window_kernel(
    win_count,
    width,
    slot_ref,
    bias_ref,
    tok_ref,
    halo_ref,
    gain_ref,
    wq_ref,
    wk_ref,
    wv_ref,
    sel_ref,
    selt_ref,
    selp_ref,
    selpt_ref,
    seln_ref,
    selnt_ref,
    mixed_ref,
    tsum_ref,
    msum_ref,
    qt_s,
    ko_s,
    ks_s,
    vo_s,
    vs_s,
    ke_s,
    ve_s,
    qz_s,
    ot_s,
):
    step = pl.program_id(0)
    groups = width // 128
    per = 128 // HDIM

    def put_side(slot, k, vt, sel, selt):
        ks = nn_dot(sel, k).astype(jnp.bfloat16)
        for g in range(groups):
            ks_s[slot, g] = ks[:, g * 128 : (g + 1) * 128]
        vs_s[slot] = nn_dot(vt, selt).astype(jnp.bfloat16)

    @pl.when(step == 0)
    def _():
        qz_s[...] = jnp.zeros_like(qz_s)
        gain = gain_ref[...]
        normed = normalize(halo_ref[...].astype(jnp.float32), gain)
        half = (HALO_WIN + 1) * STRIP
        for side, sel, selt, first in (
            (0, selp_ref, selpt_ref, 0),
            (1, seln_ref, selnt_ref, HALO_WIN + win_count),
        ):
            base = side * half
            for i in range(HALO_WIN):
                piece = jnp.concatenate(
                    [
                        normed[base + i * STRIP : base + (i + 1) * STRIP],
                        normed[base + HALO_WIN * STRIP : base + half],
                    ],
                    axis=0,
                )
                k = nn_dot(piece, wk_ref[...]).astype(jnp.bfloat16)
                vt = nt_dot(wv_ref[...], piece).astype(jnp.bfloat16)
                put_side(first + i, k, vt, sel[...], selt[...])

    @pl.when(step < win_count)
    def _():
        values = tok_ref[...].astype(jnp.float32)
        tsum_ref[0] = jnp.sum(values, axis=0, keepdims=True)
        normed = normalize(values, gain_ref[...])
        qt_s[step] = nt_dot(wq_ref[...], normed).astype(jnp.bfloat16)
        k = nn_dot(normed, wk_ref[...]).astype(jnp.bfloat16)
        for g in range(groups):
            ko_s[step, g] = k[:, g * 128 : (g + 1) * 128]
        vt = nt_dot(wv_ref[...], normed).astype(jnp.bfloat16)
        vo_s[step] = vt
        put_side(step + HALO_WIN, k, vt, sel_ref[...], selt_ref[...])

    @pl.when(step >= win_count)
    def _():
        win = step - win_count
        slots = [slot_ref[win * 8 + i] for i in range(8)]
        biases = [bias_ref[win * 8 + i] for i in range(8)]
        ke_s[:, :TOK] = ko_s[win]
        ve_s[:, :TOK] = vo_s[win]
        place = 0
        for i in range(8):
            size = STRIP if i < 4 else CORNER
            ke_s[:, TOK + place : TOK + place + size] = ks_s[slots[i], :, place : place + size]
            place += size
        lane = lax.broadcasted_iota(jnp.int32, (width, 128), 1)
        for pair in range(2):
            lo = pair * 128
            ve_s[:, TOK + lo : TOK + lo + 128] = jnp.where(
                lane < STRIP,
                vs_s[slots[2 * pair], :, lo : lo + 128],
                vs_s[slots[2 * pair + 1], :, lo : lo + 128],
            )
        corner = [vs_s[slots[4 + i], :, 256:384] for i in range(4)]
        ve_s[:, TOK + 256 : TOK + 384] = jnp.where(
            lane < 2 * CORNER,
            jnp.where(lane < CORNER, corner[0], corner[1]),
            jnp.where(lane < 3 * CORNER, corner[2], corner[3]),
        )
        for h in range(width // HDIM):
            lo = (h % per) * HDIM
            qz_s[h, lo : lo + HDIM] = qt_s[win, h * HDIM : (h + 1) * HDIM]

        factor = LOG2E / math.sqrt(HDIM)

        def group(g, carry):
            for j in range(per):
                head = g * per + j
                scores = nn_dot(ke_s[g], qz_s[head])
                parts = [scores[:TOK] * factor]
                place = TOK
                for i in range(8):
                    size = STRIP if i < 4 else CORNER
                    parts.append(scores[place : place + size] * factor + biases[i])
                    place += size
                scaled = jnp.concatenate(parts, axis=0)
                top = jnp.max(scaled, axis=0, keepdims=True)
                weights = jnp.exp2(scaled - top)
                inverse = 1.0 / jnp.sum(weights, axis=0, keepdims=True)
                probs = (weights * inverse).astype(jnp.bfloat16)
                row = pl.multiple_of(head * HDIM, HDIM)
                ot_s[pl.ds(row, HDIM), :] = nn_dot(ve_s[pl.ds(row, HDIM), :KEYS], probs)
            return carry

        lax.fori_loop(0, groups, group, 0)
        mixed = ot_s[...].T.astype(jnp.bfloat16)
        mixed_ref[...] = mixed
        msum_ref[0] = jnp.sum(mixed.astype(jnp.float32), axis=0, keepdims=True)


def window_layer(tokens, halo, gain, weight, slots, biases):
    win_count = tokens.shape[0] // TOK
    width = weight.shape[2]
    groups = width // 128
    wq, wk, wv = weight[:, 0].T, weight[:, 1], weight[:, 2].T
    tables = [t for pair in selections() for t in pair]

    def whole(array):
        return pl.BlockSpec(
            array.shape, lambda i, *_: (0,) * array.ndim, pipeline_mode=pl.Buffered(1)
        )

    def first(i, *_):
        return jnp.minimum(i, win_count - 1)

    def second(i, *_):
        return jnp.maximum(i - win_count, 0)

    fixed = [halo, gain.reshape(1, D), wq, wk, wv] + tables
    slots_n = win_count + 2 * HALO_WIN
    bf = jnp.bfloat16
    return pl.pallas_call(
        lambda *refs: window_kernel(win_count, width, *refs),
        out_shape=(
            jax.ShapeDtypeStruct((win_count * TOK, width), bf),
            jax.ShapeDtypeStruct((win_count, 1, D), jnp.float32),
            jax.ShapeDtypeStruct((win_count, 1, width), jnp.float32),
        ),
        grid_spec=pltpu.PrefetchScalarGridSpec(
            num_scalar_prefetch=2,
            grid=(2 * win_count,),
            in_specs=[pl.BlockSpec((TOK, D), lambda i, *_: (first(i), 0))]
            + [whole(a) for a in fixed],
            out_specs=(
                pl.BlockSpec((TOK, width), lambda i, *_: (second(i), 0)),
                pl.BlockSpec((1, 1, D), lambda i, *_: (first(i), 0, 0)),
                pl.BlockSpec((1, 1, width), lambda i, *_: (second(i), 0, 0)),
            ),
            scratch_shapes=[
                pltpu.VMEM((win_count, width, TOK), bf),
                pltpu.VMEM((win_count, groups, TOK, 128), bf),
                pltpu.VMEM((slots_n, groups, SIDE_KEYS, 128), bf),
                pltpu.VMEM((win_count, width, TOK), bf),
                pltpu.VMEM((slots_n, width, SIDE_LANES), bf),
                pltpu.VMEM((groups, KEYS, 128), bf),
                pltpu.VMEM((width, TOK + SIDE_LANES), bf),
                pltpu.VMEM((width // HDIM, 128, TOK), bf),
                pltpu.VMEM((width, TOK), jnp.float32),
            ],
        ),
        compiler_params=pltpu.CompilerParams(vmem_limit_bytes=58 << 20),
        cost_estimate=pl.CostEstimate(
            flops=2 * win_count * TOK * (3 * D * width + 2 * KEYS * width),
            bytes_accessed=win_count * TOK * (2 * D + 2 * width),
            transcendentals=win_count * TOK * KEYS * width // HDIM,
        ),
    )(slots.reshape(-1), biases.reshape(-1), tokens, *fixed)


def halo_tokens(tokens):
    grid = tokens.reshape(-1, WIN, WIN, D)
    count = lax.axis_size("pack")
    tail = jnp.concatenate(
        [
            grid[-HALO_WIN:, WIN - HALO :].reshape(-1, D),
            grid[-1, :, WIN - HALO :].reshape(-1, D),
        ]
    )
    head = jnp.concatenate(
        [grid[:HALO_WIN, :HALO].reshape(-1, D), grid[0, :, :HALO].reshape(-1, D)]
    )
    before = lax.ppermute(tail, "pack", [(i, i + 1) for i in range(count - 1)])
    after = lax.ppermute(head, "pack", [(i + 1, i) for i in range(count - 1)])
    return jnp.concatenate([before, after])


def layer_norm(values, gain):
    values = values.astype(jnp.float32)
    return normalize(values, gain)


def page_member(window_ids, page_windows):
    page_ends = jnp.cumsum(page_windows)
    page_starts = page_ends - page_windows
    return (window_ids[:, None] >= page_starts[None, :]) & (
        window_ids[:, None] < page_ends[None, :]
    )


def window_geometry(window_ids, page_windows, page_width):
    page_ends = jnp.cumsum(page_windows)
    page_starts = page_ends - page_windows
    member = page_member(window_ids, page_windows).astype(jnp.int32)
    begin = jnp.sum(member * page_starts[None, :], axis=1)
    across = jnp.sum(member * page_width[None, :], axis=1)
    total = jnp.sum(member * page_windows[None, :], axis=1)
    inside = window_ids - begin
    grid_row = inside // across
    grid_col = inside - grid_row * across
    rows_near = jnp.stack([grid_row + pair[0] for pair in OFFSETS], axis=1)
    cols_near = jnp.stack([grid_col + pair[1] for pair in OFFSETS], axis=1)
    place = rows_near * across[:, None] + cols_near
    valid = (
        (cols_near >= 0)
        & (cols_near < across[:, None])
        & (rows_near >= 0)
        & (place < total[:, None])
    )
    return (begin[:, None] + place, valid)


def attention(query, keys, values, mask, heads):
    qlen, width = query.shape
    depth = width // heads
    q_heads = query.reshape(qlen, heads, depth)
    k_heads = keys.reshape(-1, heads, depth)
    v_heads = values.reshape(-1, heads, depth)
    scores = jnp.einsum(
        "qhd,khd->hqk", q_heads, k_heads, preferred_element_type=jnp.float32
    ) / math.sqrt(depth)
    scores = jnp.where(mask[None], scores, -1e30)
    top_score = jnp.max(scores, axis=-1, keepdims=True)
    weights = jnp.exp(scores - top_score)
    probs = (weights / jnp.sum(weights, axis=-1, keepdims=True)).astype(jnp.bfloat16)
    output = jnp.einsum("hqk,khd->qhd", probs, v_heads, preferred_element_type=jnp.float32)
    return output.reshape(qlen, width).astype(jnp.bfloat16)


def shards(
    tokens,
    ln_gain,
    attn_weight,
    attn_proj,
    page_gain,
    page_weight,
    page_proj,
    page_windows,
    page_width,
    doc_pages,
):
    win_count = tokens.shape[0] // TOK
    local_width = attn_weight.shape[2]
    local_heads = local_width // HDIM
    offset_start = lax.axis_index("pack") * win_count
    window_ids = offset_start + jnp.arange(win_count, dtype=jnp.int32)
    neighbor, valid = window_geometry(window_ids, page_windows, page_width)
    own_index = jnp.arange(win_count, dtype=jnp.int32)[:, None] + HALO_WIN
    slots = jnp.where(valid, neighbor - offset_start + HALO_WIN, own_index)
    biases = jnp.where(valid, 0.0, -1e30).astype(jnp.float32)
    halo = halo_tokens(tokens)
    mixed, token_sums, mixed_sums = window_layer(
        tokens, halo, ln_gain, attn_weight, slots, biases
    )
    member = page_member(window_ids, page_windows).astype(jnp.float32)
    highest = lax.Precision.HIGHEST
    page_tokens = jnp.dot(member.T, token_sums[:, 0], precision=highest)
    page_mixed = jnp.dot(member.T, mixed_sums[:, 0], precision=highest)
    projected = jnp.dot(page_mixed, attn_proj.astype(jnp.float32), precision=highest)
    share = jnp.where(lax.axis_index("head") == 0, 1.0, 0.0)
    counts = TOK * page_windows.astype(jnp.float32)
    total = lax.psum(page_tokens * share + projected, ("pack", "head"))
    pooled = total / counts[:, None]
    page_count = page_windows.shape[0]
    page_normed = layer_norm(pooled, page_gain)
    page_qkv = jnp.dot(
        page_normed, page_weight.reshape(D, 3 * local_width), preferred_element_type=jnp.float32
    ).astype(jnp.bfloat16)
    doc_ends = jnp.cumsum(doc_pages)
    page_ids = jnp.arange(page_count, dtype=jnp.int32)
    doc_of = jnp.sum((page_ids[:, None] >= doc_ends[None, :]).astype(jnp.int32), axis=1)
    same_doc = doc_of[:, None] == doc_of[None, :]
    context = attention(
        page_qkv[:, :local_width],
        page_qkv[:, local_width : 2 * local_width],
        page_qkv[:, 2 * local_width :],
        same_doc,
        local_heads,
    )
    branch = jnp.dot(context, page_proj, preferred_element_type=jnp.float32)
    my_share = lax.psum_scatter(
        branch.astype(jnp.bfloat16), "head", scatter_dimension=1, tiled=True
    ).astype(jnp.float32)
    column_start = lax.axis_index("head") * my_share.shape[1]
    page_out = lax.dynamic_slice_in_dim(pooled, column_start, my_share.shape[1], 1) + my_share
    return (mixed, page_out)


def solution(mesh):
    placed = (
        P(("rep", "pack"), None),
        P(),
        P(None, None, "head"),
        P("head", None),
        P(),
        P(None, None, "head"),
        P("head", None),
        P("rep"),
        P("rep"),
        P("rep"),
    )
    return jax.shard_map(
        shards,
        mesh=mesh,
        in_specs=placed,
        out_specs=(P(("rep", "pack"), "head"), P("rep", "head")),
        check_vma=False,
    )
```

```python
import math

import jax
import jax.numpy as jnp
import numpy as np
from jax import lax
from jax.experimental import pallas as pl
from jax.experimental.pallas import tpu as pltpu
from jax.sharding import PartitionSpec as P

D = 1024
HDIM = 32
WIN = 16
HALO = 4
HALO_WIN = 4
TOK = WIN * WIN
STRIP = WIN * HALO
CORNER = HALO * HALO
SIDE_KEYS = 4 * STRIP + 4 * CORNER
KEYS = TOK + SIDE_KEYS
SIDE_LANES = 384
EPS = 1e-05
LOG2E = 1.4426950408889634
OFFSETS = ((-1, 0), (1, 0), (0, -1), (0, 1), (-1, -1), (-1, 1), (1, -1), (1, 1))


def near(offset_value):
    if offset_value < 0:
        return range(WIN - HALO, WIN)
    if offset_value > 0:
        return range(0, HALO)
    return range(0, WIN)


def strip_tokens():
    return [[r * WIN + c for r in near(a) for c in near(b)] for a, b in OFFSETS]


def one_hot(rows, width):
    table = np.zeros((SIDE_KEYS, width), np.float32)
    for i, j in enumerate(rows):
        if j >= 0:
            table[i, j] = 1.0
    padded = np.zeros((width, SIDE_LANES), np.float32)
    padded[:, :SIDE_KEYS] = table.T
    return jnp.asarray(table, jnp.bfloat16), jnp.asarray(padded, jnp.bfloat16)


def selections():
    strips = strip_tokens()
    out = [one_hot([t for s in strips for t in s], TOK)]
    for piece in (0, 1):
        where = {t: i for i, t in enumerate(strips[piece])}
        for half in (0, 1):
            rows = []
            for number, strip in enumerate(strips):
                same = OFFSETS[number][0] == OFFSETS[piece][0]
                rows += [where[t] + half * STRIP if same else -1 for t in strip]
            out.append(one_hot(rows, 2 * STRIP))
    return out


def nt_dot(a, b):
    return lax.dot_general(a, b, (((1,), (1,)), ((), ())), preferred_element_type=jnp.float32)


def nn_dot(a, b):
    return jnp.dot(a, b, preferred_element_type=jnp.float32)


def normalize(values, gain):
    center = values - jnp.mean(values, axis=-1, keepdims=True)
    spread = jnp.mean(center * center, axis=-1, keepdims=True)
    return (center * lax.rsqrt(spread + EPS) * gain).astype(jnp.bfloat16)


def window_kernel(
    win_count,
    width,
    slot_ref,
    bias_ref,
    tok_ref,
    halo_ref,
    gain_ref,
    wt_ref,
    sel_ref,
    selt_ref,
    sel00_ref,
    selt00_ref,
    sel01_ref,
    selt01_ref,
    sel10_ref,
    selt10_ref,
    sel11_ref,
    selt11_ref,
    mixed_ref,
    tsum_ref,
    msum_ref,
    qt_s,
    ko_s,
    ks_s,
    vo_s,
    vs_s,
    ke_s,
    ve_s,
    qz_s,
    ot_s,
):
    step = pl.program_id(0)
    groups = width // 128
    per = 128 // HDIM

    def put_side(slot, k, vt, sel, selt):
        ks = nn_dot(sel, k).astype(jnp.bfloat16)
        for g in range(groups):
            ks_s[slot, g] = ks[:, g * 128 : (g + 1) * 128]
        vs_s[slot] = nn_dot(vt, selt).astype(jnp.bfloat16)

    @pl.when(step == 0)
    def _():
        qz_s[...] = jnp.zeros_like(qz_s)
        normed = normalize(halo_ref[...].astype(jnp.float32), gain_ref[...])
        kvt = nt_dot(wt_ref[width:], normed).astype(jnp.bfloat16)
        k = kvt[:width].T
        half = SIDE_LANES
        for side, tables, first, edge in (
            (0, ((sel00_ref, selt00_ref), (sel01_ref, selt01_ref)), 0, HALO_WIN - 1),
            (
                1,
                ((sel10_ref, selt10_ref), (sel11_ref, selt11_ref)),
                HALO_WIN + win_count,
                HALO_WIN + win_count,
            ),
        ):
            for i in range(HALO_WIN):
                lo = side * half + (i // 2) * 128
                sel, selt = tables[i % 2]
                put_side(
                    first + i, k[lo : lo + 128], kvt[width:, lo : lo + 128], sel[...], selt[...]
                )
            lo = side * half + 2 * 128
            for g in range(groups):
                ks_s[edge, g, 2 * STRIP : 4 * STRIP] = k[lo : lo + 128, g * 128 : (g + 1) * 128]
            vs_s[edge, :, 128:256] = kvt[width:, lo : lo + 128]

    @pl.when(step < win_count)
    def _():
        values = tok_ref[...].astype(jnp.float32)
        tsum_ref[0] = jnp.sum(values, axis=0, keepdims=True)
        normed = normalize(values, gain_ref[...])
        qkvt = nt_dot(wt_ref[...], normed).astype(jnp.bfloat16)
        qt_s[step] = qkvt[:width]
        k = qkvt[width : 2 * width].T
        for g in range(groups):
            ko_s[step, g] = k[:, g * 128 : (g + 1) * 128]
        vt = qkvt[2 * width :]
        vo_s[step] = vt
        put_side(step + HALO_WIN, k, vt, sel_ref[...], selt_ref[...])

    @pl.when(step >= win_count)
    def _():
        win = step - win_count
        slots = [slot_ref[win * 8 + i] for i in range(8)]
        biases = [bias_ref[win * 8 + i] for i in range(8)]
        ke_s[:, :TOK] = ko_s[win]
        ve_s[:, :TOK] = vo_s[win]
        place = 0
        for i in range(8):
            size = STRIP if i < 4 else CORNER
            ke_s[:, TOK + place : TOK + place + size] = ks_s[slots[i], :, place : place + size]
            place += size
        lane = lax.broadcasted_iota(jnp.int32, (width, 128), 1)
        for pair in range(2):
            lo = pair * 128
            ve_s[:, TOK + lo : TOK + lo + 128] = jnp.where(
                lane < STRIP,
                vs_s[slots[2 * pair], :, lo : lo + 128],
                vs_s[slots[2 * pair + 1], :, lo : lo + 128],
            )
        corner = [vs_s[slots[4 + i], :, 256:384] for i in range(4)]
        ve_s[:, TOK + 256 : TOK + 384] = jnp.where(
            lane < 2 * CORNER,
            jnp.where(lane < CORNER, corner[0], corner[1]),
            jnp.where(lane < 3 * CORNER, corner[2], corner[3]),
        )
        for h in range(width // HDIM):
            lo = (h % per) * HDIM
            qz_s[h, lo : lo + HDIM] = qt_s[win, h * HDIM : (h + 1) * HDIM]

        factor = LOG2E / math.sqrt(HDIM)

        def group(g, carry):
            for j in range(per):
                head = g * per + j
                scores = nn_dot(ke_s[g], qz_s[head])
                parts = [scores[:TOK] * factor]
                place = TOK
                for i in range(8):
                    size = STRIP if i < 4 else CORNER
                    parts.append(scores[place : place + size] * factor + biases[i])
                    place += size
                scaled = jnp.concatenate(parts, axis=0)
                top = jnp.max(scaled, axis=0, keepdims=True)
                weights = jnp.exp2(scaled - top)
                inverse = 1.0 / jnp.sum(weights, axis=0, keepdims=True)
                row = pl.multiple_of(head * HDIM, HDIM)
                summed = nn_dot(ve_s[pl.ds(row, HDIM), :KEYS], weights.astype(jnp.bfloat16))
                ot_s[pl.ds(row, HDIM), :] = summed * inverse
            return carry

        lax.fori_loop(0, groups, group, 0, unroll=2)
        mixed = ot_s[...].T.astype(jnp.bfloat16)
        mixed_ref[...] = mixed
        msum_ref[0] = jnp.sum(mixed.astype(jnp.float32), axis=0, keepdims=True)


def window_layer(tokens, halo, gain, weight, slots, biases):
    win_count = tokens.shape[0] // TOK
    width = weight.shape[2]
    groups = width // 128
    wt = weight.reshape(D, 3 * width).T
    tables = [t for pair in selections() for t in pair]

    def whole(array):
        return pl.BlockSpec(
            array.shape, lambda i, *_: (0,) * array.ndim, pipeline_mode=pl.Buffered(1)
        )

    def first(i, *_):
        return jnp.minimum(i, win_count - 1)

    def second(i, *_):
        return jnp.maximum(i - win_count, 0)

    fixed = [halo, gain.reshape(1, D), wt] + tables
    slots_n = win_count + 2 * HALO_WIN
    bf = jnp.bfloat16
    return pl.pallas_call(
        lambda *refs: window_kernel(win_count, width, *refs),
        out_shape=(
            jax.ShapeDtypeStruct((win_count * TOK, width), bf),
            jax.ShapeDtypeStruct((win_count, 1, D), jnp.float32),
            jax.ShapeDtypeStruct((win_count, 1, width), jnp.float32),
        ),
        grid_spec=pltpu.PrefetchScalarGridSpec(
            num_scalar_prefetch=2,
            grid=(2 * win_count,),
            in_specs=[pl.BlockSpec((TOK, D), lambda i, *_: (first(i), 0))]
            + [whole(a) for a in fixed],
            out_specs=(
                pl.BlockSpec((TOK, width), lambda i, *_: (second(i), 0)),
                pl.BlockSpec((1, 1, D), lambda i, *_: (first(i), 0, 0)),
                pl.BlockSpec((1, 1, width), lambda i, *_: (second(i), 0, 0)),
            ),
            scratch_shapes=[
                pltpu.VMEM((win_count, width, TOK), bf),
                pltpu.VMEM((win_count, groups, TOK, 128), bf),
                pltpu.VMEM((slots_n, groups, SIDE_KEYS, 128), bf),
                pltpu.VMEM((win_count, width, TOK), bf),
                pltpu.VMEM((slots_n, width, SIDE_LANES), bf),
                pltpu.VMEM((groups, KEYS, 128), bf),
                pltpu.VMEM((width, TOK + SIDE_LANES), bf),
                pltpu.VMEM((width // HDIM, 128, TOK), bf),
                pltpu.VMEM((width, TOK), jnp.float32),
            ],
        ),
        compiler_params=pltpu.CompilerParams(vmem_limit_bytes=58 << 20),
        cost_estimate=pl.CostEstimate(
            flops=2 * win_count * TOK * (3 * D * width + 2 * KEYS * width),
            bytes_accessed=win_count * TOK * (2 * D + 2 * width),
            transcendentals=win_count * TOK * KEYS * width // HDIM,
        ),
    )(slots.reshape(-1), biases.reshape(-1), tokens, *fixed)


def halo_tokens(tokens):
    grid = tokens.reshape(-1, WIN, WIN, D)
    count = lax.axis_size("pack")
    tail = jnp.concatenate(
        [
            grid[-HALO_WIN:, WIN - HALO :].reshape(-1, D),
            grid[-1, :, WIN - HALO :].reshape(-1, D),
        ]
    )
    head = jnp.concatenate(
        [grid[:HALO_WIN, :HALO].reshape(-1, D), grid[0, :, :HALO].reshape(-1, D)]
    )
    before = lax.ppermute(tail, "pack", [(i, i + 1) for i in range(count - 1)])
    after = lax.ppermute(head, "pack", [(i + 1, i) for i in range(count - 1)])
    blank = jnp.zeros((STRIP, D), tokens.dtype)
    outer = HALO_WIN * STRIP
    return jnp.concatenate([before, blank, after[:outer], blank, after[outer:]])


def sum_kernel(count, heads, x_ref, out_ref, land, acc, full, send_sem, recv_sem):
    me = lax.axis_index("pack") * heads + lax.axis_index("head")

    def device(k):
        other = lax.rem(me + k, count)
        return other, {"pack": lax.div(other, heads), "head": lax.rem(other, heads)}

    barrier = pltpu.get_barrier_semaphore()

    @pl.loop(1, count)
    def _(k):
        pl.semaphore_signal(
            barrier, inc=1, device_id=device(k)[1], device_id_type=pl.DeviceIdType.MESH
        )

    pl.semaphore_wait(barrier, count - 1)

    def copy(k, phase):
        other, where = device(k)
        return pltpu.make_async_remote_copy(
            src_ref=acc if phase else x_ref.at[other],
            dst_ref=full.at[me] if phase else land.at[k],
            send_sem=send_sem.at[phase, k],
            recv_sem=recv_sem.at[phase, k],
            device_id=where,
            device_id_type=pl.DeviceIdType.MESH,
        )

    for phase in (0, 1):

        @pl.loop(1, count)
        def _(k):
            copy(k, phase).start()

        if phase:
            full[me] = acc[...]
        else:
            land[0] = x_ref[me]

        @pl.loop(1, count)
        def _(k):
            copy(k, phase).wait_recv()

        if phase:
            out_ref[...] = full[...]
        else:
            acc[...] = jnp.sum(land[...], axis=0)

    @pl.loop(1, count)
    def _(k):
        copy(k, 0).wait_send()
        copy(k, 1).wait_send()


def sum_over_devices(values):
    heads = lax.axis_size("head")
    count = lax.axis_size("pack") * heads
    rows = values.size // (count * 128)
    shape = (count, rows, 128)
    total = pl.pallas_call(
        lambda *refs: sum_kernel(count, heads, *refs),
        out_shape=jax.ShapeDtypeStruct(shape, jnp.float32),
        in_specs=[pl.BlockSpec(memory_space=pltpu.VMEM)],
        out_specs=pl.BlockSpec(memory_space=pltpu.VMEM),
        scratch_shapes=[
            pltpu.VMEM(shape, jnp.float32),
            pltpu.VMEM(shape[1:], jnp.float32),
            pltpu.VMEM(shape, jnp.float32),
            pltpu.SemaphoreType.DMA((2, count)),
            pltpu.SemaphoreType.DMA((2, count)),
        ],
        compiler_params=pltpu.CompilerParams(collective_id=0, has_side_effects=True),
    )(values.reshape(shape))
    return total.reshape(values.shape)


def keep_share(values):
    heads = lax.axis_size("head")
    me = lax.axis_index("head")
    columns = values.shape[1] // heads
    rounded = values.astype(jnp.bfloat16)

    def part(k):
        start = lax.rem(me + k, heads) * columns
        return lax.dynamic_slice_in_dim(rounded, start, columns, 1)

    total = part(0).astype(jnp.float32)
    for k in range(1, heads):
        pairs = [(i, (i + k) % heads) for i in range(heads)]
        total = total + lax.ppermute(part(k), "head", pairs).astype(jnp.float32)
    return total


def layer_norm(values, gain):
    values = values.astype(jnp.float32)
    return normalize(values, gain)


def page_member(window_ids, page_windows):
    page_ends = jnp.cumsum(page_windows)
    page_starts = page_ends - page_windows
    return (window_ids[:, None] >= page_starts[None, :]) & (
        window_ids[:, None] < page_ends[None, :]
    )


def window_geometry(window_ids, page_windows, page_width):
    page_ends = jnp.cumsum(page_windows)
    page_starts = page_ends - page_windows
    member = page_member(window_ids, page_windows).astype(jnp.int32)
    begin = jnp.sum(member * page_starts[None, :], axis=1)
    across = jnp.sum(member * page_width[None, :], axis=1)
    total = jnp.sum(member * page_windows[None, :], axis=1)
    inside = window_ids - begin
    grid_row = inside // across
    grid_col = inside - grid_row * across
    rows_near = jnp.stack([grid_row + pair[0] for pair in OFFSETS], axis=1)
    cols_near = jnp.stack([grid_col + pair[1] for pair in OFFSETS], axis=1)
    place = rows_near * across[:, None] + cols_near
    valid = (
        (cols_near >= 0)
        & (cols_near < across[:, None])
        & (rows_near >= 0)
        & (place < total[:, None])
    )
    return (begin[:, None] + place, valid)


def attention(query, keys, values, mask, heads):
    qlen, width = query.shape
    depth = width // heads
    q_heads = query.reshape(qlen, heads, depth)
    k_heads = keys.reshape(-1, heads, depth)
    v_heads = values.reshape(-1, heads, depth)
    scores = jnp.einsum(
        "qhd,khd->hqk", q_heads, k_heads, preferred_element_type=jnp.float32
    ) / math.sqrt(depth)
    scores = jnp.where(mask[None], scores, -1e30)
    top_score = jnp.max(scores, axis=-1, keepdims=True)
    weights = jnp.exp(scores - top_score)
    probs = (weights / jnp.sum(weights, axis=-1, keepdims=True)).astype(jnp.bfloat16)
    output = jnp.einsum("hqk,khd->qhd", probs, v_heads, preferred_element_type=jnp.float32)
    return output.reshape(qlen, width).astype(jnp.bfloat16)


def shards(
    tokens,
    ln_gain,
    attn_weight,
    attn_proj,
    page_gain,
    page_weight,
    page_proj,
    page_windows,
    page_width,
    doc_pages,
):
    win_count = tokens.shape[0] // TOK
    local_width = attn_weight.shape[2]
    local_heads = local_width // HDIM
    offset_start = lax.axis_index("pack") * win_count
    window_ids = offset_start + jnp.arange(win_count, dtype=jnp.int32)
    neighbor, valid = window_geometry(window_ids, page_windows, page_width)
    own_index = jnp.arange(win_count, dtype=jnp.int32)[:, None] + HALO_WIN
    slots = jnp.where(valid, neighbor - offset_start + HALO_WIN, own_index)
    biases = jnp.where(valid, 0.0, -1e30).astype(jnp.float32)
    halo = halo_tokens(tokens)
    mixed, token_sums, mixed_sums = window_layer(
        tokens, halo, ln_gain, attn_weight, slots, biases
    )
    member = page_member(window_ids, page_windows).astype(jnp.float32)
    highest = lax.Precision.HIGHEST
    page_tokens = jnp.dot(member.T, token_sums[:, 0], precision=highest)
    page_mixed = jnp.dot(member.T, mixed_sums[:, 0], precision=highest)
    projected = jnp.dot(page_mixed, attn_proj.astype(jnp.float32), precision=highest)
    share = jnp.where(lax.axis_index("head") == 0, 1.0, 0.0)
    counts = TOK * page_windows.astype(jnp.float32)
    total = sum_over_devices(page_tokens * share + projected)
    pooled = total / counts[:, None]
    page_count = page_windows.shape[0]
    page_normed = layer_norm(pooled, page_gain)
    page_qkv = jnp.dot(
        page_normed, page_weight.reshape(D, 3 * local_width), preferred_element_type=jnp.float32
    ).astype(jnp.bfloat16)
    doc_ends = jnp.cumsum(doc_pages)
    page_ids = jnp.arange(page_count, dtype=jnp.int32)
    doc_of = jnp.sum((page_ids[:, None] >= doc_ends[None, :]).astype(jnp.int32), axis=1)
    same_doc = doc_of[:, None] == doc_of[None, :]
    context = attention(
        page_qkv[:, :local_width],
        page_qkv[:, local_width : 2 * local_width],
        page_qkv[:, 2 * local_width :],
        same_doc,
        local_heads,
    )
    branch = jnp.dot(context, page_proj, preferred_element_type=jnp.float32)
    my_share = keep_share(branch)
    column_start = lax.axis_index("head") * my_share.shape[1]
    page_out = lax.dynamic_slice_in_dim(pooled, column_start, my_share.shape[1], 1) + my_share
    return (mixed, page_out)


def solution(mesh):
    placed = (
        P(("rep", "pack"), None),
        P(),
        P(None, None, "head"),
        P("head", None),
        P(),
        P(None, None, "head"),
        P("head", None),
        P("rep"),
        P("rep"),
        P("rep"),
    )
    return jax.shard_map(
        shards,
        mesh=mesh,
        in_specs=placed,
        out_specs=(P(("rep", "pack"), "head"), P("rep", "head")),
        check_vma=False,
    )
```

```python
import math

import jax
import jax.numpy as jnp
import numpy as np
from jax import lax
from jax.experimental import pallas as pl
from jax.experimental.pallas import tpu as pltpu
from jax.sharding import PartitionSpec as P

D = 1024
HDIM = 32
WIN = 16
HALO = 4
HALO_WIN = 4
TOK = WIN * WIN
STRIP = WIN * HALO
CORNER = HALO * HALO
SIDE_KEYS = 4 * STRIP + 4 * CORNER
KEYS = TOK + SIDE_KEYS
SIDE_LANES = 384
EPS = 1e-05
LOG2E = 1.4426950408889634
OFFSETS = ((-1, 0), (1, 0), (0, -1), (0, 1), (-1, -1), (-1, 1), (1, -1), (1, 1))


def near(offset_value):
    if offset_value < 0:
        return range(WIN - HALO, WIN)
    if offset_value > 0:
        return range(0, HALO)
    return range(0, WIN)


def strip_tokens():
    return [[r * WIN + c for r in near(a) for c in near(b)] for a, b in OFFSETS]


def one_hot(rows, width):
    table = np.zeros((SIDE_KEYS, width), np.float32)
    for i, j in enumerate(rows):
        if j >= 0:
            table[i, j] = 1.0
    padded = np.zeros((width, SIDE_LANES), np.float32)
    padded[:, :SIDE_KEYS] = table.T
    return jnp.asarray(table, jnp.bfloat16), jnp.asarray(padded, jnp.bfloat16)


def selections():
    strips = strip_tokens()
    out = [one_hot([t for s in strips for t in s], TOK)]
    for piece in (0, 1):
        where = {t: i for i, t in enumerate(strips[piece])}
        for half in (0, 1):
            rows = []
            for number, strip in enumerate(strips):
                same = OFFSETS[number][0] == OFFSETS[piece][0]
                rows += [where[t] + half * STRIP if same else -1 for t in strip]
            out.append(one_hot(rows, 2 * STRIP))
    return out


def nt_dot(a, b):
    return lax.dot_general(a, b, (((1,), (1,)), ((), ())), preferred_element_type=jnp.float32)


def nn_dot(a, b):
    return jnp.dot(a, b, preferred_element_type=jnp.float32)


def normalize(values, gain):
    center = values - jnp.mean(values, axis=-1, keepdims=True)
    spread = jnp.mean(center * center, axis=-1, keepdims=True)
    return (center * lax.rsqrt(spread + EPS) * gain).astype(jnp.bfloat16)


def window_kernel(
    win_count,
    width,
    slot_ref,
    bias_ref,
    tok_ref,
    halo_ref,
    gain_ref,
    wt_ref,
    sel_ref,
    selt_ref,
    sel00_ref,
    selt00_ref,
    sel01_ref,
    selt01_ref,
    sel10_ref,
    selt10_ref,
    sel11_ref,
    selt11_ref,
    mixed_ref,
    tsum_ref,
    msum_ref,
    qt_s,
    ko_s,
    ks_s,
    vo_s,
    vs_s,
    ke_s,
    ve_s,
    qz_s,
    ot_s,
):
    step = pl.program_id(0)
    groups = width // 128
    per = 128 // HDIM

    def put_side(slot, k, vt, sel, selt):
        ks = nn_dot(sel, k).astype(jnp.bfloat16)
        for g in range(groups):
            ks_s[slot, g] = ks[:, g * 128 : (g + 1) * 128]
        vs_s[slot] = nn_dot(vt, selt).astype(jnp.bfloat16)

    @pl.when(step == 0)
    def _():
        qz_s[...] = jnp.zeros_like(qz_s)
        normed = normalize(halo_ref[...].astype(jnp.float32), gain_ref[...])
        kvt = nt_dot(wt_ref[width:], normed).astype(jnp.bfloat16)
        k = kvt[:width].T
        half = SIDE_LANES
        for side, tables, first, edge in (
            (0, ((sel00_ref, selt00_ref), (sel01_ref, selt01_ref)), 0, HALO_WIN - 1),
            (
                1,
                ((sel10_ref, selt10_ref), (sel11_ref, selt11_ref)),
                HALO_WIN + win_count,
                HALO_WIN + win_count,
            ),
        ):
            for i in range(HALO_WIN):
                lo = side * half + (i // 2) * 128
                sel, selt = tables[i % 2]
                put_side(
                    first + i, k[lo : lo + 128], kvt[width:, lo : lo + 128], sel[...], selt[...]
                )
            lo = side * half + 2 * 128
            for g in range(groups):
                ks_s[edge, g, 2 * STRIP : 4 * STRIP] = k[lo : lo + 128, g * 128 : (g + 1) * 128]
            vs_s[edge, :, 128:256] = kvt[width:, lo : lo + 128]

    @pl.when(step < win_count)
    def _():
        values = tok_ref[...].astype(jnp.float32)
        tsum_ref[0] = jnp.sum(values, axis=0, keepdims=True)
        normed = normalize(values, gain_ref[...])
        qkvt = nt_dot(wt_ref[...], normed).astype(jnp.bfloat16)
        qt_s[step] = qkvt[:width]
        k = qkvt[width : 2 * width].T
        for g in range(groups):
            ko_s[step, g] = k[:, g * 128 : (g + 1) * 128]
        vt = qkvt[2 * width :]
        vo_s[step] = vt
        put_side(step + HALO_WIN, k, vt, sel_ref[...], selt_ref[...])

    @pl.when(step >= win_count)
    def _():
        win = step - win_count
        slots = [slot_ref[win * 8 + i] for i in range(8)]
        biases = [bias_ref[win * 8 + i] for i in range(8)]
        ke_s[:, :TOK] = ko_s[win]
        ve_s[:, :TOK] = vo_s[win]
        place = 0
        for i in range(8):
            size = STRIP if i < 4 else CORNER
            ke_s[:, TOK + place : TOK + place + size] = ks_s[slots[i], :, place : place + size]
            place += size
        lane = lax.broadcasted_iota(jnp.int32, (width, 128), 1)
        for pair in range(2):
            lo = pair * 128
            ve_s[:, TOK + lo : TOK + lo + 128] = jnp.where(
                lane < STRIP,
                vs_s[slots[2 * pair], :, lo : lo + 128],
                vs_s[slots[2 * pair + 1], :, lo : lo + 128],
            )
        corner = [vs_s[slots[4 + i], :, 256:384] for i in range(4)]
        ve_s[:, TOK + 256 : TOK + 384] = jnp.where(
            lane < 2 * CORNER,
            jnp.where(lane < CORNER, corner[0], corner[1]),
            jnp.where(lane < 3 * CORNER, corner[2], corner[3]),
        )
        for h in range(width // HDIM):
            lo = (h % per) * HDIM
            qz_s[h, lo : lo + HDIM] = qt_s[win, h * HDIM : (h + 1) * HDIM]

        factor = LOG2E / math.sqrt(HDIM)

        def group(g, carry):
            for j in range(per):
                head = g * per + j
                scores = nn_dot(ke_s[g], qz_s[head])
                parts = [scores[:TOK] * factor]
                place = TOK
                for i in range(8):
                    size = STRIP if i < 4 else CORNER
                    parts.append(scores[place : place + size] * factor + biases[i])
                    place += size
                scaled = jnp.concatenate(parts, axis=0)
                top = jnp.max(scaled, axis=0, keepdims=True)
                weights = jnp.exp2(scaled - top)
                inverse = 1.0 / jnp.sum(weights, axis=0, keepdims=True)
                row = pl.multiple_of(head * HDIM, HDIM)
                summed = nn_dot(ve_s[pl.ds(row, HDIM), :KEYS], weights.astype(jnp.bfloat16))
                ot_s[pl.ds(row, HDIM), :] = summed * inverse
            return carry

        lax.fori_loop(0, groups, group, 0, unroll=2)
        mixed = ot_s[...].T.astype(jnp.bfloat16)
        mixed_ref[...] = mixed
        msum_ref[0] = jnp.sum(mixed.astype(jnp.float32), axis=0, keepdims=True)


def window_layer(tokens, halo, gain, weight, slots, biases):
    win_count = tokens.shape[0] // TOK
    width = weight.shape[2]
    groups = width // 128
    wt = weight.reshape(D, 3 * width).T
    tables = [t for pair in selections() for t in pair]

    def whole(array):
        return pl.BlockSpec(
            array.shape, lambda i, *_: (0,) * array.ndim, pipeline_mode=pl.Buffered(1)
        )

    def first(i, *_):
        return jnp.minimum(i, win_count - 1)

    def second(i, *_):
        return jnp.maximum(i - win_count, 0)

    fixed = [halo, gain.reshape(1, D), wt] + tables
    slots_n = win_count + 2 * HALO_WIN
    bf = jnp.bfloat16
    return pl.pallas_call(
        lambda *refs: window_kernel(win_count, width, *refs),
        out_shape=(
            jax.ShapeDtypeStruct((win_count * TOK, width), bf),
            jax.ShapeDtypeStruct((win_count, 1, D), jnp.float32),
            jax.ShapeDtypeStruct((win_count, 1, width), jnp.float32),
        ),
        grid_spec=pltpu.PrefetchScalarGridSpec(
            num_scalar_prefetch=2,
            grid=(2 * win_count,),
            in_specs=[pl.BlockSpec((TOK, D), lambda i, *_: (first(i), 0))]
            + [whole(a) for a in fixed],
            out_specs=(
                pl.BlockSpec((TOK, width), lambda i, *_: (second(i), 0)),
                pl.BlockSpec((1, 1, D), lambda i, *_: (first(i), 0, 0)),
                pl.BlockSpec((1, 1, width), lambda i, *_: (second(i), 0, 0)),
            ),
            scratch_shapes=[
                pltpu.VMEM((win_count, width, TOK), bf),
                pltpu.VMEM((win_count, groups, TOK, 128), bf),
                pltpu.VMEM((slots_n, groups, SIDE_KEYS, 128), bf),
                pltpu.VMEM((win_count, width, TOK), bf),
                pltpu.VMEM((slots_n, width, SIDE_LANES), bf),
                pltpu.VMEM((groups, KEYS, 128), bf),
                pltpu.VMEM((width, TOK + SIDE_LANES), bf),
                pltpu.VMEM((width // HDIM, 128, TOK), bf),
                pltpu.VMEM((width, TOK), jnp.float32),
            ],
        ),
        compiler_params=pltpu.CompilerParams(vmem_limit_bytes=58 << 20),
        cost_estimate=pl.CostEstimate(
            flops=2 * win_count * TOK * (3 * D * width + 2 * KEYS * width),
            bytes_accessed=win_count * TOK * (2 * D + 2 * width),
            transcendentals=win_count * TOK * KEYS * width // HDIM,
        ),
    )(slots.reshape(-1), biases.reshape(-1), tokens, *fixed)


def halo_tokens(tokens):
    grid = tokens.reshape(-1, WIN, WIN, D)
    count = lax.axis_size("pack")
    tail = jnp.concatenate(
        [
            grid[-HALO_WIN:, WIN - HALO :].reshape(-1, D),
            grid[-1, :, WIN - HALO :].reshape(-1, D),
        ]
    )
    head = jnp.concatenate(
        [grid[:HALO_WIN, :HALO].reshape(-1, D), grid[0, :, :HALO].reshape(-1, D)]
    )
    before = lax.ppermute(tail, "pack", [(i, i + 1) for i in range(count - 1)])
    after = lax.ppermute(head, "pack", [(i + 1, i) for i in range(count - 1)])
    blank = jnp.zeros((STRIP, D), tokens.dtype)
    outer = HALO_WIN * STRIP
    return jnp.concatenate([before, blank, after[:outer], blank, after[outer:]])


def sum_kernel(wide, near_n, heads, x_ref, out_ref, land1, mid, land2, acc, row, full, sends, recvs):
    per_near = near_n // heads
    pack = lax.axis_index("pack")
    a = lax.div(pack, per_near)
    b = lax.rem(pack, per_near) * heads + lax.axis_index("head")

    def beside(k):
        other = lax.rem(b + k, near_n)
        where = {"pack": a * per_near + lax.div(other, heads), "head": lax.rem(other, heads)}
        return other, where

    def across(k):
        other = lax.rem(a + k, wide)
        where = {"pack": other * per_near + lax.rem(pack, per_near), "head": lax.axis_index("head")}
        return other, where

    barrier = pltpu.get_barrier_semaphore()
    for side, size in ((beside, near_n), (across, wide)):

        @pl.loop(1, size)
        def _(k):
            pl.semaphore_signal(
                barrier, inc=1, device_id=side(k)[1], device_id_type=pl.DeviceIdType.MESH
            )

    pl.semaphore_wait(barrier, near_n + wide - 2)

    def copy(k, stage):
        other, where = beside(k) if stage in (0, 3) else across(k)
        source = (x_ref.at[other], mid.at[other], acc, row)[stage]
        target = (land1.at[k], land2.at[k], row.at[a], full.at[b])[stage]
        return pltpu.make_async_remote_copy(
            src_ref=source,
            dst_ref=target,
            send_sem=sends.at[stage, k],
            recv_sem=recvs.at[stage, k],
            device_id=where,
            device_id_type=pl.DeviceIdType.MESH,
        )

    for stage, size in ((0, near_n), (1, wide), (2, wide), (3, near_n)):

        @pl.loop(1, size)
        def _(k):
            copy(k, stage).start()

        if stage == 0:
            land1[0] = x_ref[b]
        elif stage == 1:
            land2[0] = mid[a]
        elif stage == 2:
            row[a] = acc[...]
        else:
            full[b] = row[...]

        @pl.loop(1, size)
        def _(k):
            copy(k, stage).wait_recv()

        if stage == 0:
            mid[...] = jnp.sum(land1[...], axis=0)
        elif stage == 1:
            acc[...] = jnp.sum(land2[...], axis=0)
        elif stage == 3:
            out_ref[...] = full[...]

    for stage, size in ((0, near_n), (1, wide), (2, wide), (3, near_n)):

        @pl.loop(1, size)
        def _(k):
            copy(k, stage).wait_send()


def sum_over_devices(values):
    heads = lax.axis_size("head")
    packs = lax.axis_size("pack")
    near_n = heads * (2 if packs % 2 == 0 else 1)
    wide = packs * heads // near_n
    rows = values.size // (packs * heads * 128)
    shape = (near_n, wide, rows, 128)
    total = pl.pallas_call(
        lambda *refs: sum_kernel(wide, near_n, heads, *refs),
        out_shape=jax.ShapeDtypeStruct(shape, jnp.float32),
        in_specs=[pl.BlockSpec(memory_space=pltpu.VMEM)],
        out_specs=pl.BlockSpec(memory_space=pltpu.VMEM),
        scratch_shapes=[
            pltpu.VMEM(shape, jnp.float32),
            pltpu.VMEM(shape[1:], jnp.float32),
            pltpu.VMEM(shape[1:], jnp.float32),
            pltpu.VMEM(shape[2:], jnp.float32),
            pltpu.VMEM(shape[1:], jnp.float32),
            pltpu.VMEM(shape, jnp.float32),
            pltpu.SemaphoreType.DMA((4, max(wide, near_n))),
            pltpu.SemaphoreType.DMA((4, max(wide, near_n))),
        ],
        compiler_params=pltpu.CompilerParams(collective_id=0, has_side_effects=True),
    )(values.reshape(shape))
    return total.reshape(values.shape)


def keep_share(values):
    heads = lax.axis_size("head")
    me = lax.axis_index("head")
    columns = values.shape[1] // heads
    rounded = values.astype(jnp.bfloat16)

    def part(k):
        start = lax.rem(me + k, heads) * columns
        return lax.dynamic_slice_in_dim(rounded, start, columns, 1)

    total = part(0).astype(jnp.float32)
    for k in range(1, heads):
        pairs = [(i, (i + k) % heads) for i in range(heads)]
        total = total + lax.ppermute(part(k), "head", pairs).astype(jnp.float32)
    return total


def layer_norm(values, gain):
    values = values.astype(jnp.float32)
    return normalize(values, gain)


def page_member(window_ids, page_windows):
    page_ends = jnp.cumsum(page_windows)
    page_starts = page_ends - page_windows
    return (window_ids[:, None] >= page_starts[None, :]) & (
        window_ids[:, None] < page_ends[None, :]
    )


def window_geometry(window_ids, page_windows, page_width):
    page_ends = jnp.cumsum(page_windows)
    page_starts = page_ends - page_windows
    member = page_member(window_ids, page_windows).astype(jnp.int32)
    begin = jnp.sum(member * page_starts[None, :], axis=1)
    across = jnp.sum(member * page_width[None, :], axis=1)
    total = jnp.sum(member * page_windows[None, :], axis=1)
    inside = window_ids - begin
    grid_row = inside // across
    grid_col = inside - grid_row * across
    rows_near = jnp.stack([grid_row + pair[0] for pair in OFFSETS], axis=1)
    cols_near = jnp.stack([grid_col + pair[1] for pair in OFFSETS], axis=1)
    place = rows_near * across[:, None] + cols_near
    valid = (
        (cols_near >= 0)
        & (cols_near < across[:, None])
        & (rows_near >= 0)
        & (place < total[:, None])
    )
    return (begin[:, None] + place, valid)


def attention(query, keys, values, mask, heads):
    qlen, width = query.shape
    depth = width // heads
    q_heads = query.reshape(qlen, heads, depth)
    k_heads = keys.reshape(-1, heads, depth)
    v_heads = values.reshape(-1, heads, depth)
    scores = jnp.einsum(
        "qhd,khd->hqk", q_heads, k_heads, preferred_element_type=jnp.float32
    ) / math.sqrt(depth)
    scores = jnp.where(mask[None], scores, -1e30)
    top_score = jnp.max(scores, axis=-1, keepdims=True)
    weights = jnp.exp(scores - top_score)
    probs = (weights / jnp.sum(weights, axis=-1, keepdims=True)).astype(jnp.bfloat16)
    output = jnp.einsum("hqk,khd->qhd", probs, v_heads, preferred_element_type=jnp.float32)
    return output.reshape(qlen, width).astype(jnp.bfloat16)


def shards(
    tokens,
    ln_gain,
    attn_weight,
    attn_proj,
    page_gain,
    page_weight,
    page_proj,
    page_windows,
    page_width,
    doc_pages,
):
    win_count = tokens.shape[0] // TOK
    local_width = attn_weight.shape[2]
    local_heads = local_width // HDIM
    offset_start = lax.axis_index("pack") * win_count
    window_ids = offset_start + jnp.arange(win_count, dtype=jnp.int32)
    neighbor, valid = window_geometry(window_ids, page_windows, page_width)
    own_index = jnp.arange(win_count, dtype=jnp.int32)[:, None] + HALO_WIN
    slots = jnp.where(valid, neighbor - offset_start + HALO_WIN, own_index)
    biases = jnp.where(valid, 0.0, -1e30).astype(jnp.float32)
    halo = halo_tokens(tokens)
    mixed, token_sums, mixed_sums = window_layer(
        tokens, halo, ln_gain, attn_weight, slots, biases
    )
    member = page_member(window_ids, page_windows).astype(jnp.float32)
    highest = lax.Precision.HIGHEST
    page_tokens = jnp.dot(member.T, token_sums[:, 0], precision=highest)
    page_mixed = jnp.dot(member.T, mixed_sums[:, 0], precision=highest)
    projected = jnp.dot(page_mixed, attn_proj.astype(jnp.float32), precision=highest)
    share = jnp.where(lax.axis_index("head") == 0, 1.0, 0.0)
    counts = TOK * page_windows.astype(jnp.float32)
    total = sum_over_devices(page_tokens * share + projected)
    pooled = total / counts[:, None]
    page_count = page_windows.shape[0]
    page_normed = layer_norm(pooled, page_gain)
    page_qkv = jnp.dot(
        page_normed, page_weight.reshape(D, 3 * local_width), preferred_element_type=jnp.float32
    ).astype(jnp.bfloat16)
    doc_ends = jnp.cumsum(doc_pages)
    page_ids = jnp.arange(page_count, dtype=jnp.int32)
    doc_of = jnp.sum((page_ids[:, None] >= doc_ends[None, :]).astype(jnp.int32), axis=1)
    same_doc = doc_of[:, None] == doc_of[None, :]
    context = attention(
        page_qkv[:, :local_width],
        page_qkv[:, local_width : 2 * local_width],
        page_qkv[:, 2 * local_width :],
        same_doc,
        local_heads,
    )
    branch = jnp.dot(context, page_proj, preferred_element_type=jnp.float32)
    my_share = keep_share(branch)
    column_start = lax.axis_index("head") * my_share.shape[1]
    page_out = lax.dynamic_slice_in_dim(pooled, column_start, my_share.shape[1], 1) + my_share
    return (mixed, page_out)


def solution(mesh):
    placed = (
        P(("rep", "pack"), None),
        P(),
        P(None, None, "head"),
        P("head", None),
        P(),
        P(None, None, "head"),
        P("head", None),
        P("rep"),
        P("rep"),
        P("rep"),
    )
    return jax.shard_map(
        shards,
        mesh=mesh,
        in_specs=placed,
        out_specs=(P(("rep", "pack"), "head"), P("rep", "head")),
        check_vma=False,
    )
```
